32 devices in a mesh: grp: 2 (over x), comp: 16 (over z, y, core).
Axes of the slice: x: 2, y: 2, z: 4, core: 2. Of those that a mesh axis runs over, the one named last changes fastest.
Arguments:
- spectrum: float32 [1152, 96, 128], P(None, ('grp', 'comp')), parts along dimension 1, may hold values from 0.04 to 14, as said below
- sea_mask: int32 [96, 128], P(('grp', 'comp')), parts along dimension 0, may hold values 0 or 1
- ice_mask: int32 [96, 128], P(('grp', 'comp')), parts along dimension 0, may hold values 0 or 1
- wind: float32 [96, 128], P(('grp', 'comp')), parts along dimension 0, may hold values from 0.2 to 1
- source_matrix: bfloat16 [1152, 1152], replicated, may hold values from -0.1875 to 0.1875
Outputs:
- evolved: float32 [1152, 96, 128], P(None, ('grp', 'comp')), parts along dimension 1
The draws below stay inside these ranges and needn't reach their ends.
There are 2 independent parts, one for each index of `grp`. The reference program is written for one: setup_inputs(seed, part) draws one part's arguments, and reference() takes and returns one part's arrays. A program takes and returns all parts, laid end to end along the dimension named above; an argument that names none is the same for every part. Nothing has to cross between parts.
Inputs may be any that keep to these rules, and one draw needn't show every extreme that they name: `spectrum`: positive spectral densities.
All inputs are finite; a program needn't handle non-finite values. No bound on the sum of `sea_mask` or of `ice_mask` on one device may be relied on, other than what follows from the above.
Results may differ from the reference program's by a relative error of at most 0.0014.
Values sent between devices are 32-bit elements; how exact they have to be, the bound alone decides.
A program may use at most 64 MiB of HBM per device.

```python
import math
import jax
import jax.numpy as jnp

NDIR = 36
NFREQ = 32
K = 1152
NX = 128
NY = 48
STEPS = 2
SUBSTEPS = 3
SRC_SUB = 3


def draw_spectrum(key, part):
    base_key = jax.random.fold_in(key, 11)
    first_key, second_key, third_key = jax.random.split(base_key, 3)
    baseline = jax.random.uniform(first_key, (K, NY, NX), jnp.float32, 0.5, 1.5)
    cell_scale = jnp.exp(jax.random.uniform(second_key, (1, NY, NX), jnp.float32, math.log(0.3), math.log(3.0)))
    comp_scale = jnp.exp(jax.random.uniform(third_key, (K, 1, 1), jnp.float32, math.log(0.3), math.log(3.0)))
    return baseline * cell_scale * comp_scale


def with_ends(result, stream_key, least, high):
    dims = result.shape
    spot = [jax.random.randint(jax.random.fold_in(stream_key, axis), (), 0, dims[axis]) for axis in range(len(dims))]
    result = result.at[tuple(spot)].set(least)
    longest = dims.index(max(dims))
    spot[longest] = (spot[longest] + 1) % dims[longest]
    return result.at[tuple(spot)].set(high)


def levels(rng, dims, shards, low, high):
    def one(dim, blocks):
        heights = jax.random.uniform(jax.random.fold_in(jax.random.fold_in(rng, 6), dim), (blocks,), jnp.float32, low / len(shards), high / len(shards))
        return jnp.repeat(jnp.exp(heights), dims[dim] // blocks).reshape((-1,) + (1,) * (len(dims) - dim - 1))

    loudness = one(*shards[0])
    for cut in shards[1:]:
        loudness = loudness * one(*cut)
    return loudness


def centred(key, extent, deviation, limit, kind=jnp.bfloat16):
    values = jax.random.normal(key, extent, jnp.float32) * deviation
    return jnp.minimum(jnp.maximum(values, -limit), limit).astype(kind)


def setup_inputs(seed: int = 0, part: int = 0) -> dict:
    arg_keys = jax.random.split(jax.random.key(seed), 6)
    part_splits = jax.random.split(jax.random.fold_in(arg_keys[5], part), 6)
    spectrum = draw_spectrum(jax.random.fold_in(jax.random.fold_in(arg_keys[5], part), 71), part)
    sea_mask = with_ends((jax.random.randint(part_splits[1], (NY, NX), 0, 8) < 7).astype(jnp.int32), jax.random.fold_in(part_splits[1], 1), 0, 1)
    ice_mask = with_ends((jax.random.randint(part_splits[2], (NY, NX), 0, 6) < 1).astype(jnp.int32), jax.random.fold_in(part_splits[2], 1), 0, 1)
    wind = jnp.clip(0.2 + 0.8 * jax.random.uniform(part_splits[3], (NY, NX), jnp.float32) ** levels(part_splits[3], (NY, NX), ((0, 16),), -0.2, 0.2), 0.2, 1.0)
    source_matrix = centred(arg_keys[4], (K, K), K ** -0.5, 0.1875)
    return dict(spectrum=spectrum, sea_mask=sea_mask, ice_mask=ice_mask, wind=wind, source_matrix=source_matrix)


source_rate = 0.5
damping = 0.5


def courant(comp_index):
    direction = (comp_index % NDIR).astype(jnp.float32)
    frequency = (comp_index // NDIR).astype(jnp.float32)
    angles = 2.0 * jnp.pi * (direction + 0.5) / NDIR
    speeds = 0.6 * (0.35 + 0.65 * (NFREQ - 1 - frequency) / (NFREQ - 1))
    return (speeds * jnp.cos(angles))[:, None, None], (speeds * jnp.sin(angles))[:, None, None]


def advance(spectra, courant_x, courant_y):
    western = jnp.roll(spectra, 1, axis=2)
    eastern = jnp.roll(spectra, -1, axis=2)
    zero_row = jnp.zeros_like(spectra[:, :1])
    southern = jnp.concatenate([zero_row, spectra[:, :-1]], axis=1)
    northern = jnp.concatenate([spectra[:, 1:], zero_row], axis=1)
    staying = 1.0 - jnp.abs(courant_x) - jnp.abs(courant_y)
    return (staying * spectra + jnp.maximum(courant_x, 0.0) * western + jnp.maximum(-courant_x, 0.0) * eastern
            + jnp.maximum(courant_y, 0.0) * southern + jnp.maximum(-courant_y, 0.0) * northern)


def sources(spectra, sea, wind, source_matrix):
    layout_shape = spectra.shape
    flattened = spectra.reshape(layout_shape[0], -1)
    sea_flat = sea.reshape(1, -1)
    wind_flat = wind.reshape(1, -1)
    for source_step in range(SRC_SUB):
        rounded = flattened.astype(jnp.bfloat16)
        growth = jnp.dot(source_matrix, rounded, preferred_element_type=jnp.float32)
        energy = jnp.mean(flattened * flattened, axis=0, keepdims=True)
        flattened = sea_flat * (flattened + source_rate * wind_flat * growth) / (1.0 + damping * energy)
    return flattened.reshape(layout_shape)


def reference(spectrum, sea_mask, ice_mask, wind, source_matrix):
    sea = sea_mask.astype(jnp.float32)
    thaw = (1.0 - 0.5 * ice_mask.astype(jnp.float32))[None]
    courant_x, courant_y = courant(jnp.arange(K, dtype=jnp.int32))
    spectra = spectrum
    for outer_step in range(STEPS):
        for inner_step in range(SUBSTEPS):
            spectra = sea[None] * advance(spectra, courant_x, courant_y)
        spectra = sources(spectra, sea, wind, source_matrix) * thaw
    return spectra
```

```python
import functools

import jax
import jax.numpy as jnp
import numpy as np
from jax import lax
from jax.experimental import pallas as pl
from jax.experimental.pallas import tpu as pltpu
from jax.sharding import PartitionSpec as P

NDIR = 36
NFREQ = 32
K = NDIR * NFREQ
STEPS = 2
SUBSTEPS = 3
SRC_SUB = 3
RATE = 0.5
DAMPING = 0.5

HALF = NDIR // 2
FREQS = 4
GROUP = FREQS * NDIR
SIDE = GROUP // 2
GROUPS = K // GROUP
BLOCK = 24
TILE = 288
MESH = pl.DeviceIdType.MESH


def packed_order():
    inside = np.arange(GROUP).reshape(FREQS, 2, HALF).transpose(1, 0, 2).reshape(-1)
    return inside, (np.arange(GROUPS)[:, None] * GROUP + inside).reshape(-1)


def coefficients(order):
    direction = (order % NDIR).astype(np.float32)
    frequency = (order // NDIR).astype(np.float32)
    angles = (2.0 * np.pi * (direction + 0.5) / NDIR).astype(np.float64)
    speeds = 0.6 * (0.35 + 0.65 * (NFREQ - 1 - frequency.astype(np.float64)) / (NFREQ - 1))
    cx, cy = speeds * np.cos(angles), speeds * np.sin(angles)
    cx, cy = cx.astype(np.float32), cy.astype(np.float32)
    staying = np.float32(1.0) - np.abs(cx) - np.abs(cy)
    return np.stack([staying, cx, np.abs(cy)], axis=1).astype(np.float32)


def pieces():
    for j in range(FREQS):
        for side in range(2):
            yield j * NDIR + side * HALF, side * SIDE + j * HALF


def kernel(size, spec, sea_ref, ice_ref, wind_ref, mat, coef_hbm, lanes_ref, subs_ref, out,
           nat, first, second, work, south, north, sea_south, sea_north, mat_nat, mat_packed, onehot,
           coef, low, total, load_sem, mat_sem, coef_sem, mask_send, mask_recv, up_send, up_recv,
           down_send, down_recv, out_sem):
    rows, width = spec.shape[0], spec.shape[2]
    me = lax.axis_index("comp")
    has_south, has_north = me > 0, me < size - 1

    loads = []
    for g in range(GROUPS):
        part = pl.ds(g * GROUP, GROUP)
        copy = pltpu.make_async_copy(spec.at[:, part, :], nat.at[:, part, :], load_sem.at[g])
        copy.start()
        loads.append(copy)
    mat_load = pltpu.make_async_copy(mat, mat_nat, mat_sem)
    mat_load.start()
    coef_load = pltpu.make_async_copy(coef_hbm, coef, coef_sem)
    coef_load.start()

    barrier = pltpu.get_barrier_semaphore()

    @pl.when(has_south)
    def _():
        pl.semaphore_signal(barrier, inc=1, device_id={"comp": me - 1}, device_id_type=MESH)

    @pl.when(has_north)
    def _():
        pl.semaphore_signal(barrier, inc=1, device_id={"comp": me + 1}, device_id_type=MESH)

    def up_copy(buffer, step, g):
        return pltpu.make_async_remote_copy(
            src_ref=buffer.at[pl.ds(rows - SUBSTEPS, SUBSTEPS), pl.ds(g * GROUP, SIDE), :],
            dst_ref=south.at[step, :, pl.ds(g * SIDE, SIDE), :],
            send_sem=up_send.at[step, g], recv_sem=up_recv.at[step, g],
            device_id={"comp": me + 1}, device_id_type=MESH)

    def down_copy(buffer, step, g):
        return pltpu.make_async_remote_copy(
            src_ref=buffer.at[pl.ds(0, SUBSTEPS), pl.ds(g * GROUP + SIDE, SIDE), :],
            dst_ref=north.at[step, :, pl.ds(g * SIDE, SIDE), :],
            send_sem=down_send.at[step, g], recv_sem=down_recv.at[step, g],
            device_id={"comp": me - 1}, device_id_type=MESH)

    def send(buffer, step, g):
        @pl.when(has_north)
        def _():
            up_copy(buffer, step, g).start()

        @pl.when(has_south)
        def _():
            down_copy(buffer, step, g).start()

    def mask_up():
        return pltpu.make_async_remote_copy(
            src_ref=sea_ref, dst_ref=sea_south, send_sem=mask_send.at[0], recv_sem=mask_recv.at[0],
            device_id={"comp": me + 1}, device_id_type=MESH)

    def mask_down():
        return pltpu.make_async_remote_copy(
            src_ref=sea_ref, dst_ref=sea_north, send_sem=mask_send.at[1], recv_sem=mask_recv.at[1],
            device_id={"comp": me - 1}, device_id_type=MESH)

    for g in range(GROUPS):
        loads[g].wait()
        for r in range(rows):
            for natural, packed in pieces():
                first[r, pl.ds(g * GROUP + packed, HALF), :] = nat[r, pl.ds(g * GROUP + natural, HALF), :]
        if g == 0:
            pl.semaphore_wait(barrier, has_south.astype(jnp.int32) + has_north.astype(jnp.int32))

            @pl.when(has_north)
            def _():
                mask_up().start()

            @pl.when(has_south)
            def _():
                mask_down().start()
        else:
            send(first, 0, g - 1)
    @pl.when(jnp.logical_not(has_south))
    def _():
        sea_south[...] = jnp.zeros_like(sea_south)
        south[...] = jnp.zeros_like(south)

    @pl.when(jnp.logical_not(has_north))
    def _():
        sea_north[...] = jnp.zeros_like(sea_north)
        north[...] = jnp.zeros_like(north)

    send(first, 0, GROUPS - 1)

    inner = (lax.broadcasted_iota(jnp.int32, (GROUP, GROUP), 1) == subs_ref[...])
    inner = inner.astype(jnp.float32).astype(jnp.bfloat16)

    def one_rows(i, carry):
        start = pl.multiple_of(i * GROUP, GROUP)
        line = lax.broadcasted_iota(jnp.int32, (GROUP, K), 0) + start
        onehot[pl.ds(start, GROUP), :] = (line == lanes_ref[...]).astype(jnp.float32).astype(jnp.bfloat16)
        return carry

    lax.fori_loop(0, GROUPS, one_rows, 0)
    mat_load.wait()
    third = K // 3

    def reorder(i, carry):
        start = pl.multiple_of(i * TILE, TILE)
        for c in range(3):
            columns = pl.ds(c * third, third)
            moved = jnp.dot(mat_nat[pl.ds(start, TILE), :], onehot[:, columns],
                            preferred_element_type=jnp.float32).astype(jnp.bfloat16)
            for s in range(TILE // GROUP):
                mat_packed[pl.ds(start + s * GROUP, GROUP), columns] = jnp.dot(
                    inner, moved[s * GROUP:(s + 1) * GROUP], preferred_element_type=jnp.float32
                ).astype(jnp.bfloat16)
        return carry

    lax.fori_loop(0, K // TILE, reorder, 0)
    coef_load.wait()

    @pl.when(has_south)
    def _():
        mask_up().wait_recv()

    @pl.when(has_north)
    def _():
        mask_down().wait_recv()

    sea = [sea_ref[pl.ds(r, 1), :].astype(jnp.float32) for r in range(rows)]
    sea_below = [sea_south[pl.ds(rows - SUBSTEPS + r, 1), :].astype(jnp.float32) for r in range(SUBSTEPS)]
    sea_above = [sea_north[pl.ds(r, 1), :].astype(jnp.float32) for r in range(SUBSTEPS)]
    thaw = [1.0 - 0.5 * ice_ref[pl.ds(r, 1), :].astype(jnp.float32) for r in range(rows)]
    gain = [RATE * wind_ref[pl.ds(r, 1), :] for r in range(rows)]

    def upwind(lines, seas, at):
        staying = coef[pl.ds(at, BLOCK), 0:1]
        cx = coef[pl.ds(at, BLOCK), 1:2]
        cy = jnp.broadcast_to(coef[pl.ds(at, BLOCK), 2:3], lines[0].shape)
        staying = jnp.broadcast_to(staying, lines[0].shape)
        cx = jnp.broadcast_to(cx, lines[0].shape)
        eastward, cx = cx > 0.0, jnp.abs(cx)
        for _ in range(SUBSTEPS):
            moved = []
            for i in range(1, len(lines)):
                side = jnp.where(eastward, pltpu.roll(lines[i], 1, 1), pltpu.roll(lines[i], width - 1, 1))
                moved.append(seas[i] * (staying * lines[i] + cx * side + cy * lines[i - 1]))
            lines, seas = moved, seas[1:]
        return lines

    def fold(value):
        return jnp.sum(value.reshape(-1, 8, width), axis=0)

    for step in range(STEPS):
        source = first if step == 0 else second
        for r in range(rows):
            total[r] = jnp.zeros((8, width), jnp.float32)
        for g in range(GROUPS):
            @pl.when(has_south)
            def _():
                up_copy(source, step, g).wait_recv()

            @pl.when(has_north)
            def _():
                down_copy(source, step, g).wait_recv()

            def block(i, carry):
                at = pl.multiple_of(g * GROUP + i * BLOCK, 8)
                halo = pl.multiple_of(g * SIDE + i * BLOCK, 8)
                lines = [south[step, r, pl.ds(halo, BLOCK), :] for r in range(SUBSTEPS)]
                lines += [source[r, pl.ds(at, BLOCK), :] for r in range(rows)]
                lines = upwind(lines, sea_below + sea, at)
                for r in range(rows):
                    work[r, pl.ds(at, BLOCK), :] = lines[r]
                at = pl.multiple_of(at + SIDE, 8)
                lines = [north[step, r, pl.ds(halo, BLOCK), :] for r in reversed(range(SUBSTEPS))]
                lines += [source[r, pl.ds(at, BLOCK), :] for r in reversed(range(rows))]
                lines = upwind(lines, (sea + sea_above)[::-1], at)
                for r in range(rows):
                    work[r, pl.ds(at, BLOCK), :] = lines[rows - 1 - r]
                return carry

            lax.fori_loop(0, SIDE // BLOCK, block, 0)
            for r in range(rows):
                value = work[r, pl.ds(g * GROUP, GROUP), :]
                low[0, pl.ds(g * GROUP, GROUP), pl.ds(r * width, width)] = value.astype(jnp.bfloat16)
                total[r] += fold(value * value)

        @pl.when(has_north)
        def _():
            for g in range(GROUPS):
                up_copy(source, step, g).wait_send()

        @pl.when(has_south)
        def _():
            for g in range(GROUPS):
                down_copy(source, step, g).wait_send()

        for sub in range(SRC_SUB):
            now, later = sub % 2, (sub + 1) % 2
            last = sub == SRC_SUB - 1
            scale = []
            for r in range(rows):
                energy = jnp.sum(total[r], axis=0, keepdims=True) * (1.0 / K)
                factor = sea[r] / (1.0 + DAMPING * energy)
                scale.append(factor * thaw[r] if last else factor)
                total[r] = jnp.zeros((8, width), jnp.float32)
            for t in range(K // TILE):
                part = pl.ds(t * TILE, TILE)
                growth = jnp.dot(mat_packed[part, :], low[now], preferred_element_type=jnp.float32)
                for r in range(rows):
                    value = (work[r, part, :] + gain[r] * growth[:, r * width:(r + 1) * width]) * scale[r]
                    if last:
                        second[r, part, :] = value
                    else:
                        work[r, part, :] = value
                        low[later, part, pl.ds(r * width, width)] = value.astype(jnp.bfloat16)
                        total[r] += fold(value * value)
                if last and step < STEPS - 1:
                    if t > 0:
                        for g in range((t - 1) * TILE // GROUP, t * TILE // GROUP):
                            send(second, step + 1, g)
                if last and step == STEPS - 1:
                    for g in range(t * TILE // GROUP, (t + 1) * TILE // GROUP):
                        for r in range(rows):
                            for natural, packed in pieces():
                                nat[r, pl.ds(g * GROUP + natural, HALF), :] = second[
                                    r, pl.ds(g * GROUP + packed, HALF), :]
                        area = pl.ds(g * GROUP, GROUP)
                        pltpu.make_async_copy(nat.at[:, area, :], out.at[:, area, :], out_sem.at[g]).start()
            if last and step < STEPS - 1:
                for g in range((K - TILE) // GROUP, GROUPS):
                    send(second, step + 1, g)
        if step == 0:
            @pl.when(has_north)
            def _():
                mask_up().wait_send()

            @pl.when(has_south)
            def _():
                mask_down().wait_send()

    for g in range(GROUPS):
        area = pl.ds(g * GROUP, GROUP)
        pltpu.make_async_copy(nat.at[:, area, :], out.at[:, area, :], out_sem.at[g]).wait()


def on_device(spectrum, sea_mask, ice_mask, wind, source_matrix):
    size = lax.axis_size("comp")
    spectra = spectrum.transpose(1, 0, 2)
    rows, _, width = spectra.shape
    inside, order = packed_order()
    coef = jnp.asarray(coefficients(order))
    lanes = jnp.asarray(order.astype(np.int32)[None, :])
    subs = jnp.asarray(inside.astype(np.int32)[:, None])
    hbm = pl.BlockSpec(memory_space=pl.ANY)
    vmem = pl.BlockSpec(memory_space=pltpu.VMEM)
    dma = pltpu.SemaphoreType.DMA
    full = pltpu.VMEM((rows, K, width), jnp.float32)
    result = pl.pallas_call(
        functools.partial(kernel, size),
        out_shape=jax.ShapeDtypeStruct(spectra.shape, jnp.float32),
        in_specs=[hbm, vmem, vmem, vmem, hbm, hbm, vmem, vmem],
        out_specs=hbm,
        scratch_shapes=[
            full, full, full, full,
            pltpu.VMEM((STEPS, SUBSTEPS, K // 2, width), jnp.float32),
            pltpu.VMEM((STEPS, SUBSTEPS, K // 2, width), jnp.float32),
            pltpu.VMEM(sea_mask.shape, jnp.int32),
            pltpu.VMEM(sea_mask.shape, jnp.int32),
            pltpu.VMEM((K, K), jnp.bfloat16),
            pltpu.VMEM((K, K), jnp.bfloat16),
            pltpu.VMEM((K, K), jnp.bfloat16),
            pltpu.VMEM(coef.shape, jnp.float32),
            pltpu.VMEM((2, K, rows * width), jnp.bfloat16),
            pltpu.VMEM((rows, 8, width), jnp.float32),
            dma((GROUPS,)), dma, dma, dma((2,)), dma((2,)),
            dma((STEPS, GROUPS)), dma((STEPS, GROUPS)), dma((STEPS, GROUPS)), dma((STEPS, GROUPS)),
            dma((GROUPS,)),
        ],
        compiler_params=pltpu.CompilerParams(
            collective_id=0, has_side_effects=True, vmem_limit_bytes=56 * 1024 * 1024),
        name="wave",
    )(spectra, sea_mask, ice_mask, wind, source_matrix, coef, lanes, subs)
    return result.transpose(1, 0, 2)


def solution(mesh):
    return jax.shard_map(
        on_device,
        mesh=mesh,
        in_specs=(
            P(None, ("grp", "comp"), None),
            P(("grp", "comp"), None),
            P(("grp", "comp"), None),
            P(("grp", "comp"), None),
            P(),
        ),
        out_specs=P(None, ("grp", "comp"), None),
        check_vma=False,
    )
```

```python
import functools

import jax
import jax.numpy as jnp
import numpy as np
from jax import lax
from jax.experimental import pallas as pl
from jax.experimental.pallas import tpu as pltpu
from jax.sharding import PartitionSpec as P

NDIR = 36
NFREQ = 32
K = NDIR * NFREQ
STEPS = 2
SUBSTEPS = 3
SRC_SUB = 3
RATE = 0.5
DAMPING = 0.5

HALF = NDIR // 2
FREQS = 4
GROUP = FREQS * NDIR
SIDE = GROUP // 2
GROUPS = K // GROUP
BLOCK = 24
TILE = 288
MESH = pl.DeviceIdType.MESH


def packed_order():
    inside = np.arange(GROUP).reshape(FREQS, 2, HALF).transpose(1, 0, 2).reshape(-1)
    return inside, (np.arange(GROUPS)[:, None] * GROUP + inside).reshape(-1)


def coefficients(order):
    direction = (order % NDIR).astype(np.float32)
    frequency = (order // NDIR).astype(np.float32)
    angles = (2.0 * np.pi * (direction + 0.5) / NDIR).astype(np.float64)
    speeds = 0.6 * (0.35 + 0.65 * (NFREQ - 1 - frequency.astype(np.float64)) / (NFREQ - 1))
    cx, cy = speeds * np.cos(angles), speeds * np.sin(angles)
    cx, cy = cx.astype(np.float32), cy.astype(np.float32)
    staying = np.float32(1.0) - np.abs(cx) - np.abs(cy)
    return np.stack([staying, cx, np.abs(cy)], axis=1).astype(np.float32)


def pieces():
    for j in range(FREQS):
        for side in range(2):
            yield j * NDIR + side * HALF, side * SIDE + j * HALF


def kernel(size, spec, sea_ref, ice_ref, wind_ref, mat, coef_hbm, lanes_ref, subs_ref, out,
           nat, first, second, work, south, north, sea_south, sea_north, mat_nat, mat_packed, onehot,
           coef, low_middle, low_edges, last_rows, total, load_sem, mat_sem, coef_sem, mask_send, mask_recv, up_send, up_recv,
           down_send, down_recv, out_sem):
    rows, width = spec.shape[0], spec.shape[2]
    me = lax.axis_index("comp")
    has_south, has_north = me > 0, me < size - 1

    loads = []
    for g in range(GROUPS):
        part = pl.ds(g * GROUP, GROUP)
        copy = pltpu.make_async_copy(spec.at[:, part, :], nat.at[:, part, :], load_sem.at[g])
        copy.start()
        loads.append(copy)
    mat_load = pltpu.make_async_copy(mat, mat_nat, mat_sem)
    mat_load.start()
    coef_load = pltpu.make_async_copy(coef_hbm, coef, coef_sem)
    coef_load.start()

    barrier = pltpu.get_barrier_semaphore()

    @pl.when(has_south)
    def _():
        pl.semaphore_signal(barrier, inc=1, device_id={"comp": me - 1}, device_id_type=MESH)

    @pl.when(has_north)
    def _():
        pl.semaphore_signal(barrier, inc=1, device_id={"comp": me + 1}, device_id_type=MESH)

    def up_copy(buffer, step, far, g):
        return pltpu.make_async_remote_copy(
            src_ref=buffer.at[rows - 1 - far, pl.ds(g * GROUP, SIDE), :],
            dst_ref=south.at[step, SUBSTEPS - 1 - far, pl.ds(g * SIDE, SIDE), :],
            send_sem=up_send.at[step, far, g], recv_sem=up_recv.at[step, far, g],
            device_id={"comp": me + 1}, device_id_type=MESH)

    def down_copy(buffer, step, far, g):
        return pltpu.make_async_remote_copy(
            src_ref=buffer.at[far, pl.ds(g * GROUP + SIDE, SIDE), :],
            dst_ref=north.at[step, far, pl.ds(g * SIDE, SIDE), :],
            send_sem=down_send.at[step, far, g], recv_sem=down_recv.at[step, far, g],
            device_id={"comp": me - 1}, device_id_type=MESH)

    def each(groups, act):
        def once(i, carry):
            act(groups[0] + i)
            return carry

        if len(groups) == 1:
            act(groups[0])
        else:
            lax.fori_loop(0, len(groups), once, 0)

    def send(buffer, step, far, groups):
        @pl.when(has_north)
        def _():
            each(groups, lambda g: up_copy(buffer, step, far, g).start())

        @pl.when(has_south)
        def _():
            each(groups, lambda g: down_copy(buffer, step, far, g).start())

    def mask_up():
        return pltpu.make_async_remote_copy(
            src_ref=sea_ref, dst_ref=sea_south, send_sem=mask_send.at[0], recv_sem=mask_recv.at[0],
            device_id={"comp": me + 1}, device_id_type=MESH)

    def mask_down():
        return pltpu.make_async_remote_copy(
            src_ref=sea_ref, dst_ref=sea_north, send_sem=mask_send.at[1], recv_sem=mask_recv.at[1],
            device_id={"comp": me - 1}, device_id_type=MESH)

    for g in range(GROUPS):
        loads[g].wait()
        for r in range(rows):
            for natural, packed in pieces():
                first[r, pl.ds(g * GROUP + packed, HALF), :] = nat[r, pl.ds(g * GROUP + natural, HALF), :]
        if g == 0:
            pl.semaphore_wait(barrier, has_south.astype(jnp.int32) + has_north.astype(jnp.int32))

            @pl.when(has_north)
            def _():
                mask_up().start()

            @pl.when(has_south)
            def _():
                mask_down().start()
        else:
            send(first, 0, 0, (g - 1,))
    send(first, 0, 0, (GROUPS - 1,))
    for far in range(1, SUBSTEPS):
        send(first, 0, far, range(GROUPS))

    @pl.when(jnp.logical_not(has_south))
    def _():
        sea_south[...] = jnp.zeros_like(sea_south)
        south[...] = jnp.zeros_like(south)

    @pl.when(jnp.logical_not(has_north))
    def _():
        sea_north[...] = jnp.zeros_like(sea_north)
        north[...] = jnp.zeros_like(north)

    inner = (lax.broadcasted_iota(jnp.int32, (GROUP, GROUP), 1) == subs_ref[...])
    inner = inner.astype(jnp.float32).astype(jnp.bfloat16)

    def one_rows(i, carry):
        start = pl.multiple_of(i * GROUP, GROUP)
        line = lax.broadcasted_iota(jnp.int32, (GROUP, K), 0) + start
        onehot[pl.ds(start, GROUP), :] = (line == lanes_ref[...]).astype(jnp.float32).astype(jnp.bfloat16)
        return carry

    lax.fori_loop(0, GROUPS, one_rows, 0)
    mat_load.wait()
    third = K // 3

    def reorder(i, carry):
        start = pl.multiple_of(i * TILE, TILE)
        for c in range(3):
            columns = pl.ds(c * third, third)
            moved = jnp.dot(mat_nat[pl.ds(start, TILE), :], onehot[:, columns],
                            preferred_element_type=jnp.float32).astype(jnp.bfloat16)
            for s in range(TILE // GROUP):
                mat_packed[pl.ds(start + s * GROUP, GROUP), columns] = jnp.dot(
                    inner, moved[s * GROUP:(s + 1) * GROUP], preferred_element_type=jnp.float32
                ).astype(jnp.bfloat16)
        return carry

    lax.fori_loop(0, K // TILE, reorder, 0)
    coef_load.wait()

    @pl.when(has_south)
    def _():
        mask_up().wait_recv()

    @pl.when(has_north)
    def _():
        mask_down().wait_recv()

    sea = [sea_ref[pl.ds(r, 1), :].astype(jnp.float32) for r in range(rows)]
    sea_below = [sea_south[pl.ds(rows - SUBSTEPS + r, 1), :].astype(jnp.float32) for r in range(SUBSTEPS)]
    sea_above = [sea_north[pl.ds(r, 1), :].astype(jnp.float32) for r in range(SUBSTEPS)]
    thaw = [1.0 - 0.5 * ice_ref[pl.ds(r, 1), :].astype(jnp.float32) for r in range(rows)]
    gain = [RATE * wind_ref[pl.ds(r, 1), :] for r in range(rows)]

    def upwind(lines, seas, at):
        shape = lines[0].shape
        staying = jnp.broadcast_to(coef[pl.ds(at, BLOCK), 0:1], shape)
        cx = jnp.broadcast_to(coef[pl.ds(at, BLOCK), 1:2], shape)
        cy = jnp.broadcast_to(coef[pl.ds(at, BLOCK), 2:3], shape)
        eastward, cx = cx > 0.0, jnp.abs(cx)
        for _ in range(SUBSTEPS):
            moved = []
            for i in range(1, len(lines)):
                side = jnp.where(eastward, pltpu.roll(lines[i], 1, 1), pltpu.roll(lines[i], width - 1, 1))
                moved.append(seas[i] * (staying * lines[i] + cx * side + cy * lines[i - 1]))
            lines, seas = moved, seas[1:]
        return lines[0]

    def fold(value):
        return jnp.sum(value.reshape(-1, 8, width), axis=0)

    def advance_rows(source, step, far):
        upper, lower = rows - 1 - far, far
        def group(g, carry):
            @pl.when(has_south)
            def _():
                up_copy(source, step, far, g).wait_recv()

            @pl.when(has_north)
            def _():
                down_copy(source, step, far, g).wait_recv()

            for i in range(SIDE // BLOCK):
                at = pl.multiple_of(g * GROUP + i * BLOCK, 8)
                halo = pl.multiple_of(g * SIDE + i * BLOCK, 8)
                lines = [south[step, SUBSTEPS - 1 - f, pl.ds(halo, BLOCK), :] for f in range(far, -1, -1)]
                lines += [source[r, pl.ds(at, BLOCK), :] for r in range(upper + 1)]
                seas = (sea_below + sea)[upper:upper + SUBSTEPS + 1]
                work[upper, pl.ds(at, BLOCK), :] = upwind(lines, seas, at)
                at = pl.multiple_of(at + SIDE, 8)
                lines = [north[step, f, pl.ds(halo, BLOCK), :] for f in range(far, -1, -1)]
                lines += [source[r, pl.ds(at, BLOCK), :] for r in range(rows - 1, lower - 1, -1)]
                seas = (sea + sea_above)[lower:lower + SUBSTEPS + 1][::-1]
                work[lower, pl.ds(at, BLOCK), :] = upwind(lines, seas, at)
            return carry

        lax.fori_loop(0, GROUPS, group, 0)

    def prepare(chosen, low):
        for j, r in enumerate(chosen):
            total[r] = jnp.zeros((8, width), jnp.float32)
            for t in range(K // TILE):
                value = work[r, pl.ds(t * TILE, TILE), :]
                low[0, pl.ds(t * TILE, TILE), pl.ds(j * width, width)] = value.astype(jnp.bfloat16)
                total[r] += fold(value * value)

    def grow(chosen, low, step, fars):
        target = second if step < STEPS - 1 else last_rows
        for sub in range(SRC_SUB):
            now, later = sub % 2, (sub + 1) % 2
            last = sub == SRC_SUB - 1
            scale = {}
            for r in chosen:
                energy = jnp.sum(total[r], axis=0, keepdims=True) * (1.0 / K)
                factor = sea[r] / (1.0 + DAMPING * energy)
                scale[r] = factor * thaw[r] if last else factor
                total[r] = jnp.zeros((8, width), jnp.float32)
            def tile(t):
                part = pl.ds(pl.multiple_of(t * TILE, 16), TILE)
                growth = jnp.dot(mat_packed[part, :], low[now], preferred_element_type=jnp.float32)
                for j, r in enumerate(chosen):
                    value = (work[r, part, :] + gain[r] * growth[:, j * width:(j + 1) * width]) * scale[r]
                    if last:
                        target[r, part, :] = value
                    else:
                        work[r, part, :] = value
                        low[later, part, pl.ds(j * width, width)] = value.astype(jnp.bfloat16)
                        total[r] += fold(value * value)

            if len(chosen) == 1:
                each(range(K // TILE), tile)
                if last and step < STEPS - 1:
                    send(second, step + 1, fars[0], range(GROUPS))
            else:
                for t in range(K // TILE):
                    tile(t)
                    if last and step < STEPS - 1 and t > 0:
                        send(second, step + 1, fars[0], range((t - 1) * TILE // GROUP, t * TILE // GROUP))
            if last and step == STEPS - 1:
                each(range(GROUPS), lambda g: unpack(chosen, g))
        if step < STEPS - 1 and len(chosen) > 1:
            send(second, step + 1, fars[0], range((K - TILE) // GROUP, GROUPS))
            send(second, step + 1, fars[1], range(GROUPS))

    def unpack(chosen, g):
        start = pl.multiple_of(g * GROUP, 8)
        for r in chosen:
            value = last_rows[r, pl.ds(start, GROUP), :]
            nat[r, pl.ds(start, GROUP), :] = jnp.concatenate(
                [value[packed:packed + HALF] for _, packed in pieces()], axis=0)
            give(r, g).start()

    def give(r, g):
        area = pl.ds(g * GROUP, GROUP)
        return pltpu.make_async_copy(nat.at[r, area, :], out.at[r, area, :], out_sem.at[r, g])

    for step in range(STEPS):
        source = first if step == 0 else second
        advance_rows(source, step, 0)
        advance_rows(source, step, 1)
        middle, edges = [1], [0, rows - 1]
        prepare(middle, low_middle)
        grow(middle, low_middle, step, (1,))
        advance_rows(source, step, 2)
        prepare(edges, low_edges)
        grow(edges, low_edges, step, (0, 2))

    @pl.when(has_north)
    def _():
        mask_up().wait_send()
        for step in range(STEPS):
            for far in range(SUBSTEPS):
                each(range(GROUPS), lambda g: up_copy(
                    first if step == 0 else second, step, far, g).wait_send())

    @pl.when(has_south)
    def _():
        mask_down().wait_send()
        for step in range(STEPS):
            for far in range(SUBSTEPS):
                each(range(GROUPS), lambda g: down_copy(
                    first if step == 0 else second, step, far, g).wait_send())

    for r in range(rows):
        each(range(GROUPS), lambda g: give(r, g).wait())


def on_device(spectrum, sea_mask, ice_mask, wind, source_matrix):
    size = lax.axis_size("comp")
    spectra = spectrum.transpose(1, 0, 2)
    rows, _, width = spectra.shape
    inside, order = packed_order()
    coef = jnp.asarray(coefficients(order))
    lanes = jnp.asarray(order.astype(np.int32)[None, :])
    subs = jnp.asarray(inside.astype(np.int32)[:, None])
    hbm = pl.BlockSpec(memory_space=pl.ANY)
    vmem = pl.BlockSpec(memory_space=pltpu.VMEM)
    dma = pltpu.SemaphoreType.DMA
    link = dma((STEPS, SUBSTEPS, GROUPS))
    full = pltpu.VMEM((rows, K, width), jnp.float32)
    result = pl.pallas_call(
        functools.partial(kernel, size),
        out_shape=jax.ShapeDtypeStruct(spectra.shape, jnp.float32),
        in_specs=[hbm, vmem, vmem, vmem, hbm, hbm, vmem, vmem],
        out_specs=hbm,
        scratch_shapes=[
            full, full, full, full,
            pltpu.VMEM((STEPS, SUBSTEPS, K // 2, width), jnp.float32),
            pltpu.VMEM((STEPS, SUBSTEPS, K // 2, width), jnp.float32),
            pltpu.VMEM(sea_mask.shape, jnp.int32),
            pltpu.VMEM(sea_mask.shape, jnp.int32),
            pltpu.VMEM((K, K), jnp.bfloat16),
            pltpu.VMEM((K, K), jnp.bfloat16),
            pltpu.VMEM((K, K), jnp.bfloat16),
            pltpu.VMEM(coef.shape, jnp.float32),
            pltpu.VMEM((2, K, width), jnp.bfloat16),
            pltpu.VMEM((2, K, 2 * width), jnp.bfloat16),
            full,
            pltpu.VMEM((rows, 8, width), jnp.float32),
            dma((GROUPS,)), dma, dma, dma((2,)), dma((2,)),
            link, link, link, link,
            dma((rows, GROUPS)),
        ],
        compiler_params=pltpu.CompilerParams(
            collective_id=0, has_side_effects=True, vmem_limit_bytes=56 * 1024 * 1024),
        name="wave",
    )(spectra, sea_mask, ice_mask, wind, source_matrix, coef, lanes, subs)
    return result.transpose(1, 0, 2)


def solution(mesh):
    return jax.shard_map(
        on_device,
        mesh=mesh,
        in_specs=(
            P(None, ("grp", "comp"), None),
            P(("grp", "comp"), None),
            P(("grp", "comp"), None),
            P(("grp", "comp"), None),
            P(),
        ),
        out_specs=P(None, ("grp", "comp"), None),
        check_vma=False,
    )
```

```python
import functools

import jax
import jax.numpy as jnp
import numpy as np
from jax import lax
from jax.experimental import pallas as pl
from jax.experimental.pallas import tpu as pltpu
from jax.sharding import PartitionSpec as P

NDIR = 36
NFREQ = 32
K = NDIR * NFREQ
STEPS = 2
SUBSTEPS = 3
SRC_SUB = 3
RATE = 0.5
DAMPING = 0.5

QUARTER = NDIR // 4
FREQS = 8
GROUP = FREQS * NDIR
SIDE = GROUP // 2
PART = GROUP // 4
GROUPS = K // GROUP
BLOCK = 24
TILE = 288
MESH = pl.DeviceIdType.MESH


def packed_order():
    inside = np.arange(GROUP).reshape(FREQS, 4, QUARTER).transpose(1, 0, 2).reshape(-1)
    return inside, (np.arange(GROUPS)[:, None] * GROUP + inside).reshape(-1)


def coefficients(order):
    direction = (order % NDIR).astype(np.float32)
    frequency = (order // NDIR).astype(np.float32)
    angles = (2.0 * np.pi * (direction + 0.5) / NDIR).astype(np.float64)
    speeds = 0.6 * (0.35 + 0.65 * (NFREQ - 1 - frequency.astype(np.float64)) / (NFREQ - 1))
    cx, cy = speeds * np.cos(angles), speeds * np.sin(angles)
    cx, cy = cx.astype(np.float32), cy.astype(np.float32)
    staying = np.float32(1.0) - np.abs(cx) - np.abs(cy)
    return np.stack([staying, np.abs(cx), np.abs(cy)], axis=1).astype(np.float32)


def pieces():
    for j in range(FREQS):
        for quarter in range(4):
            yield j * NDIR + quarter * QUARTER, (quarter * FREQS + j) * QUARTER


def kernel(size, spec, sea_ref, ice_ref, wind_ref, mat, coef_hbm, lanes_ref, subs_ref, out,
           nat, first, second, work, south, north, sea_south, sea_north, mat_nat, mat_packed, onehot,
           coef, low, total, load_sem, mat_sem, coef_sem, mask_send, mask_recv, up_send, up_recv,
           down_send, down_recv, out_sem):
    rows, width = spec.shape[0], spec.shape[2]
    me = lax.axis_index("comp")
    has_south, has_north = me > 0, me < size - 1

    loads = []
    for g in range(GROUPS):
        part = pl.ds(g * GROUP, GROUP)
        copy = pltpu.make_async_copy(spec.at[:, part, :], nat.at[:, part, :], load_sem.at[g])
        copy.start()
        loads.append(copy)
    mat_load = pltpu.make_async_copy(mat, mat_nat, mat_sem)
    mat_load.start()
    coef_load = pltpu.make_async_copy(coef_hbm, coef, coef_sem)
    coef_load.start()

    barrier = pltpu.get_barrier_semaphore()

    @pl.when(has_south)
    def _():
        pl.semaphore_signal(barrier, inc=1, device_id={"comp": me - 1}, device_id_type=MESH)

    @pl.when(has_north)
    def _():
        pl.semaphore_signal(barrier, inc=1, device_id={"comp": me + 1}, device_id_type=MESH)

    def up_copy(buffer, step, g):
        return pltpu.make_async_remote_copy(
            src_ref=buffer.at[pl.ds(rows - SUBSTEPS, SUBSTEPS), pl.ds(g * GROUP, SIDE), :],
            dst_ref=south.at[step, :, pl.ds(g * SIDE, SIDE), :],
            send_sem=up_send.at[step, g], recv_sem=up_recv.at[step, g],
            device_id={"comp": me + 1}, device_id_type=MESH)

    def down_copy(buffer, step, g):
        return pltpu.make_async_remote_copy(
            src_ref=buffer.at[pl.ds(0, SUBSTEPS), pl.ds(g * GROUP + SIDE, SIDE), :],
            dst_ref=north.at[step, :, pl.ds(g * SIDE, SIDE), :],
            send_sem=down_send.at[step, g], recv_sem=down_recv.at[step, g],
            device_id={"comp": me - 1}, device_id_type=MESH)

    def send(buffer, step, g):
        @pl.when(has_north)
        def _():
            up_copy(buffer, step, g).start()

        @pl.when(has_south)
        def _():
            down_copy(buffer, step, g).start()

    def mask_up():
        return pltpu.make_async_remote_copy(
            src_ref=sea_ref, dst_ref=sea_south, send_sem=mask_send.at[0], recv_sem=mask_recv.at[0],
            device_id={"comp": me + 1}, device_id_type=MESH)

    def mask_down():
        return pltpu.make_async_remote_copy(
            src_ref=sea_ref, dst_ref=sea_north, send_sem=mask_send.at[1], recv_sem=mask_recv.at[1],
            device_id={"comp": me - 1}, device_id_type=MESH)

    for g in range(GROUPS):
        loads[g].wait()
        for r in range(rows):
            for natural, packed in pieces():
                first[r, pl.ds(g * GROUP + packed, QUARTER), :] = nat[r, pl.ds(g * GROUP + natural, QUARTER), :]
        if g == 0:
            pl.semaphore_wait(barrier, has_south.astype(jnp.int32) + has_north.astype(jnp.int32))

            @pl.when(has_north)
            def _():
                mask_up().start()

            @pl.when(has_south)
            def _():
                mask_down().start()
        else:
            send(first, 0, g - 1)
    @pl.when(jnp.logical_not(has_south))
    def _():
        sea_south[...] = jnp.zeros_like(sea_south)
        south[...] = jnp.zeros_like(south)

    @pl.when(jnp.logical_not(has_north))
    def _():
        sea_north[...] = jnp.zeros_like(sea_north)
        north[...] = jnp.zeros_like(north)

    send(first, 0, GROUPS - 1)

    inner = (lax.broadcasted_iota(jnp.int32, (GROUP, GROUP), 1) == subs_ref[...])
    inner = inner.astype(jnp.float32).astype(jnp.bfloat16)

    def one_rows(i, carry):
        start = pl.multiple_of(i * GROUP, GROUP)
        line = lax.broadcasted_iota(jnp.int32, (GROUP, K), 0) + start
        onehot[pl.ds(start, GROUP), :] = (line == lanes_ref[...]).astype(jnp.float32).astype(jnp.bfloat16)
        return carry

    lax.fori_loop(0, GROUPS, one_rows, 0)
    mat_load.wait()
    third = K // 3

    def reorder(i, carry):
        start = pl.multiple_of(i * TILE, TILE)
        for c in range(3):
            columns = pl.ds(c * third, third)
            moved = jnp.dot(mat_nat[pl.ds(start, TILE), :], onehot[:, columns],
                            preferred_element_type=jnp.float32).astype(jnp.bfloat16)
            for s in range(TILE // GROUP):
                mat_packed[pl.ds(start + s * GROUP, GROUP), columns] = jnp.dot(
                    inner, moved[s * GROUP:(s + 1) * GROUP], preferred_element_type=jnp.float32
                ).astype(jnp.bfloat16)
        return carry

    lax.fori_loop(0, K // TILE, reorder, 0)
    coef_load.wait()

    @pl.when(has_south)
    def _():
        mask_up().wait_recv()

    @pl.when(has_north)
    def _():
        mask_down().wait_recv()

    sea = [sea_ref[pl.ds(r, 1), :].astype(jnp.float32) for r in range(rows)]
    sea_below = [sea_south[pl.ds(rows - SUBSTEPS + r, 1), :].astype(jnp.float32) for r in range(SUBSTEPS)]
    sea_above = [sea_north[pl.ds(r, 1), :].astype(jnp.float32) for r in range(SUBSTEPS)]
    thaw = [1.0 - 0.5 * ice_ref[pl.ds(r, 1), :].astype(jnp.float32) for r in range(rows)]
    gain = [RATE * wind_ref[pl.ds(r, 1), :] for r in range(rows)]

    def upwind(lines, seas, at, shift):
        staying = coef[pl.ds(at, BLOCK), 0:1]
        cx = coef[pl.ds(at, BLOCK), 1:2]
        cy = jnp.broadcast_to(coef[pl.ds(at, BLOCK), 2:3], lines[0].shape)
        staying = jnp.broadcast_to(staying, lines[0].shape)
        cx = jnp.broadcast_to(cx, lines[0].shape)
        for _ in range(SUBSTEPS):
            moved = []
            for i in range(1, len(lines)):
                side = pltpu.roll(lines[i], shift, 1)
                moved.append(seas[i] * (staying * lines[i] + cx * side + cy * lines[i - 1]))
            lines, seas = moved, seas[1:]
        return lines

    def fold(value):
        return jnp.sum(value.reshape(-1, 8, width), axis=0)

    for step in range(STEPS):
        source = first if step == 0 else second
        for r in range(rows):
            total[r] = jnp.zeros((8, width), jnp.float32)
        for g in range(GROUPS):
            @pl.when(has_south)
            def _():
                up_copy(source, step, g).wait_recv()

            @pl.when(has_north)
            def _():
                down_copy(source, step, g).wait_recv()

            def block(i, carry):
                for quarter, shift in ((0, 1), (1, width - 1)):
                    halo = pl.multiple_of(g * SIDE + quarter * PART + i * BLOCK, 8)
                    at = pl.multiple_of(g * GROUP + quarter * PART + i * BLOCK, 8)
                    lines = [south[step, r, pl.ds(halo, BLOCK), :] for r in range(SUBSTEPS)]
                    lines += [source[r, pl.ds(at, BLOCK), :] for r in range(rows)]
                    lines = upwind(lines, sea_below + sea, at, shift)
                    for r in range(rows):
                        work[r, pl.ds(at, BLOCK), :] = lines[r]
                for quarter, shift in ((0, width - 1), (1, 1)):
                    halo = pl.multiple_of(g * SIDE + quarter * PART + i * BLOCK, 8)
                    at = pl.multiple_of(g * GROUP + SIDE + quarter * PART + i * BLOCK, 8)
                    lines = [north[step, r, pl.ds(halo, BLOCK), :] for r in reversed(range(SUBSTEPS))]
                    lines += [source[r, pl.ds(at, BLOCK), :] for r in reversed(range(rows))]
                    lines = upwind(lines, (sea + sea_above)[::-1], at, shift)
                    for r in range(rows):
                        work[r, pl.ds(at, BLOCK), :] = lines[rows - 1 - r]
                return carry

            lax.fori_loop(0, PART // BLOCK, block, 0)
            for r in range(rows):
                value = work[r, pl.ds(g * GROUP, GROUP), :]
                low[0, pl.ds(g * GROUP, GROUP), pl.ds(r * width, width)] = value.astype(jnp.bfloat16)
                total[r] += fold(value * value)

        @pl.when(has_north)
        def _():
            for g in range(GROUPS):
                up_copy(source, step, g).wait_send()

        @pl.when(has_south)
        def _():
            for g in range(GROUPS):
                down_copy(source, step, g).wait_send()

        for sub in range(SRC_SUB):
            now, later = sub % 2, (sub + 1) % 2
            last = sub == SRC_SUB - 1
            scale = []
            for r in range(rows):
                energy = jnp.sum(total[r], axis=0, keepdims=True) * (1.0 / K)
                factor = sea[r] / (1.0 + DAMPING * energy)
                scale.append(factor * thaw[r] if last else factor)
                total[r] = jnp.zeros((8, width), jnp.float32)
            for t in range(K // TILE):
                part = pl.ds(t * TILE, TILE)
                growth = jnp.dot(mat_packed[part, :], low[now], preferred_element_type=jnp.float32)
                for r in range(rows):
                    value = (work[r, part, :] + gain[r] * growth[:, r * width:(r + 1) * width]) * scale[r]
                    if last:
                        second[r, part, :] = value
                    else:
                        work[r, part, :] = value
                        low[later, part, pl.ds(r * width, width)] = value.astype(jnp.bfloat16)
                        total[r] += fold(value * value)
                if last and step < STEPS - 1:
                    if t > 0:
                        for g in range((t - 1) * TILE // GROUP, t * TILE // GROUP):
                            send(second, step + 1, g)
                if last and step == STEPS - 1:
                    for g in range(t * TILE // GROUP, (t + 1) * TILE // GROUP):
                        for r in range(rows):
                            for natural, packed in pieces():
                                nat[r, pl.ds(g * GROUP + natural, QUARTER), :] = second[
                                    r, pl.ds(g * GROUP + packed, QUARTER), :]
                        area = pl.ds(g * GROUP, GROUP)
                        pltpu.make_async_copy(nat.at[:, area, :], out.at[:, area, :], out_sem.at[g]).start()
            if last and step < STEPS - 1:
                for g in range((K - TILE) // GROUP, GROUPS):
                    send(second, step + 1, g)
        if step == 0:
            @pl.when(has_north)
            def _():
                mask_up().wait_send()

            @pl.when(has_south)
            def _():
                mask_down().wait_send()

    for g in range(GROUPS):
        area = pl.ds(g * GROUP, GROUP)
        pltpu.make_async_copy(nat.at[:, area, :], out.at[:, area, :], out_sem.at[g]).wait()


def on_device(spectrum, sea_mask, ice_mask, wind, source_matrix):
    size = lax.axis_size("comp")
    spectra = spectrum.transpose(1, 0, 2)
    rows, _, width = spectra.shape
    inside, order = packed_order()
    coef = jnp.asarray(coefficients(order))
    lanes = jnp.asarray(order.astype(np.int32)[None, :])
    subs = jnp.asarray(inside.astype(np.int32)[:, None])
    hbm = pl.BlockSpec(memory_space=pl.ANY)
    vmem = pl.BlockSpec(memory_space=pltpu.VMEM)
    dma = pltpu.SemaphoreType.DMA
    full = pltpu.VMEM((rows, K, width), jnp.float32)
    result = pl.pallas_call(
        functools.partial(kernel, size),
        out_shape=jax.ShapeDtypeStruct(spectra.shape, jnp.float32),
        in_specs=[hbm, vmem, vmem, vmem, hbm, hbm, vmem, vmem],
        out_specs=hbm,
        scratch_shapes=[
            full, full, full, full,
            pltpu.VMEM((STEPS, SUBSTEPS, K // 2, width), jnp.float32),
            pltpu.VMEM((STEPS, SUBSTEPS, K // 2, width), jnp.float32),
            pltpu.VMEM(sea_mask.shape, jnp.int32),
            pltpu.VMEM(sea_mask.shape, jnp.int32),
            pltpu.VMEM((K, K), jnp.bfloat16),
            pltpu.VMEM((K, K), jnp.bfloat16),
            pltpu.VMEM((K, K), jnp.bfloat16),
            pltpu.VMEM(coef.shape, jnp.float32),
            pltpu.VMEM((2, K, rows * width), jnp.bfloat16),
            pltpu.VMEM((rows, 8, width), jnp.float32),
            dma((GROUPS,)), dma, dma, dma((2,)), dma((2,)),
            dma((STEPS, GROUPS)), dma((STEPS, GROUPS)), dma((STEPS, GROUPS)), dma((STEPS, GROUPS)),
            dma((GROUPS,)),
        ],
        compiler_params=pltpu.CompilerParams(
            collective_id=0, has_side_effects=True, vmem_limit_bytes=56 * 1024 * 1024),
        name="wave",
    )(spectra, sea_mask, ice_mask, wind, source_matrix, coef, lanes, subs)
    return result.transpose(1, 0, 2)


def solution(mesh):
    return jax.shard_map(
        on_device,
        mesh=mesh,
        in_specs=(
            P(None, ("grp", "comp"), None),
            P(("grp", "comp"), None),
            P(("grp", "comp"), None),
            P(("grp", "comp"), None),
            P(),
        ),
        out_specs=P(None, ("grp", "comp"), None),
        check_vma=False,
    )
```
